256 devices in a mesh: wide: 16 (over z_lo, x, core), long: 16 (over y, z_hi).
Axes of the slice: x: 4, y: 4, z: 8 (z_hi: 4, z_lo: 2; z = z_hi * 2 + z_lo), core: 2. Of those that a mesh axis runs over, the one named last changes fastest.
Arguments:
- slab_vertices: float32 [3, 4096], P(None, 'wide'), may hold values from 0 to 1
- slab_elements: int32 [3, 8192], P(None, 'wide'), may hold values from 0 to 4095, as said below
- source_vertices: float32 [3, 16384], P(None, ('wide', 'long')), may hold values from 0 to 1
- source_elements: int32 [3, 32768], P(None, ('wide', 'long')), may hold values from 0 to 16383, as said below
- primal_basis: bfloat16 [32, 32768], P(None, ('wide', 'long')), may hold values from -12 to 12
- adjoint_basis: bfloat16 [32, 8192], P(None, 'wide'), may hold values from -24 to 24
Outputs:
- primal_image: float32 [32, 8192], P(None, ('wide', 'long'))
- adjoint_image: float32 [32, 32768], P(None, ('wide', 'long'))
The draws below stay inside these ranges and needn't reach their ends.
Inputs may be any that keep to these rules, and one draw needn't show every extreme that they name: `slab_elements`: a slab triangle in columns b * 512 to (b + 1) * 512 - 1 names only vertices b * 256 to (b + 1) * 256 - 1; both ends of each such range are named. `source_elements`: a source triangle in columns b * 128 to (b + 1) * 128 - 1 names only vertices b * 64 to (b + 1) * 64 - 1; both ends of each such range are named.
All inputs are finite; a program needn't handle non-finite values.
Results may differ from the reference program's by a relative error of at most 0.0029.
Values may be sent and summed in bfloat16 or wider, within the bound.
A program may use at most 64 MiB of HBM per device.

```python
import math
import jax
import jax.numpy as jnp
from jax import lax

BASIS = 16
SLAB_W = 512
SRC_DEV = 128
SLAB = 8192
SOURCES = 32768


def block_connectivity(key, total, block):
    half_block = block // 2
    columns = jnp.arange(total, dtype=jnp.int32)[None, :]
    corner_row = jnp.arange(3, dtype=jnp.int32)[:, None]
    base_ids = columns // block * half_block
    offsets = jax.random.randint(jax.random.fold_in(key, 17), (3, total), 0, half_block, dtype=jnp.int32)
    values = base_ids + offsets
    values = jnp.where((corner_row == 0) & (columns % block == 0), base_ids, values)
    values = jnp.where((corner_row == 2) & (columns % block == block - 1), base_ids + half_block - 1, values)
    return values


def draw_slab_elements(key, part):
    return block_connectivity(key, SLAB, SLAB_W)


def draw_source_elements(key, part):
    return block_connectivity(key, SOURCES, SRC_DEV)


def block_scale(rng, dims, split, least, largest):
    loudness, own = 1.0, jax.random.fold_in(rng, 6)
    for position, blocks in split:
        heights = jnp.exp(jax.random.uniform(jax.random.fold_in(own, position), (blocks,), jnp.float32, least / len(split), largest / len(split)))
        loudness = loudness * jnp.repeat(heights, dims[position] // blocks).reshape([-1 if axis == position else 1 for axis in range(len(dims))])
    return loudness


def normal_values(own_key, shape, scale, limit, cuts=(), kind=jnp.bfloat16):
    values = scale * jax.random.normal(own_key, shape, jnp.float32)
    if cuts:
        values = values * block_scale(own_key, shape, cuts, -0.22, 0.18)
    return jnp.clip(values, -limit, limit).astype(kind)


def setup_inputs(seed: int = 0) -> dict:
    key_list = jax.random.split(jax.random.key(seed), 7)
    return {
        "slab_vertices": jnp.clip(1.0 * jax.random.uniform(key_list[0], (3, SLAB // 2), jnp.float32) ** block_scale(key_list[0], (3, SLAB // 2), ((1, 16),), -0.2, 0.2), 0.0, 1.0),
        "slab_elements": draw_slab_elements(jax.random.fold_in(key_list[6], 71), 0),
        "source_vertices": jnp.clip(1.0 * jax.random.uniform(key_list[2], (3, SOURCES // 2), jnp.float32) ** block_scale(key_list[2], (3, SOURCES // 2), ((1, 256),), -0.2, 0.2), 0.0, 1.0),
        "source_elements": draw_source_elements(jax.random.fold_in(key_list[6], 71), 0),
        "primal_basis": normal_values(key_list[4], (2 * BASIS, SOURCES), 2.0, 12.0, ((1, 256),)),
        "adjoint_basis": normal_values(key_list[5], (2 * BASIS, SLAB), 4.0, 24.0, ((1, 16),)),
    }


WAVENUMBER = 40.0
SOFTENING = 0.0004
AREA_WEIGHT = 0.05
FOUR_PI = 4.0 * math.pi

def geometry(vertices, elements):
    corners = [jnp.take(vertices, elements[corner], axis=1) for corner in range(3)]
    centre = (corners[0] + corners[1] + corners[2]) / 3.0
    edge_one = corners[1] - corners[0]
    edge_two = corners[2] - corners[0]
    normal_x = edge_one[1] * edge_two[2] - edge_one[2] * edge_two[1]
    normal_y = edge_one[2] * edge_two[0] - edge_one[0] * edge_two[2]
    normal_z = edge_one[0] * edge_two[1] - edge_one[1] * edge_two[0]
    areas = 0.5 * jnp.sqrt(normal_x * normal_x + normal_y * normal_y + normal_z * normal_z)
    return jnp.concatenate([centre, areas[None, :]], axis=0)

def kernel_tile(targets, sources):
    spread = targets[0][:, None] - sources[0][None, :]
    square_sum = spread * spread
    for axis_id in range(1, 3):
        spread = targets[axis_id][:, None] - sources[axis_id][None, :]
        square_sum = square_sum + spread * spread
    radius = jnp.sqrt(square_sum + SOFTENING + AREA_WEIGHT * (targets[3][:, None] + sources[3][None, :]))
    weight = targets[3][:, None] * sources[3][None, :] / (FOUR_PI * radius)
    phases = WAVENUMBER * radius
    return ((weight * jnp.cos(phases)).astype(jnp.bfloat16), (weight * jnp.sin(phases)).astype(jnp.bfloat16))

def pack_primal(columns):
    half_rows = columns.shape[0] // 2
    real_part = columns[:half_rows]
    imag_part = columns[half_rows:]
    return jnp.concatenate([jnp.concatenate([real_part, -imag_part], 1), jnp.concatenate([imag_part, real_part], 1)], 0)

def pack_adjoint(row_block):
    half_rows = row_block.shape[0] // 2
    real_part = row_block[:half_rows]
    imag_part = row_block[half_rows:]
    return jnp.concatenate([jnp.concatenate([real_part, imag_part], 1), jnp.concatenate([imag_part, -real_part], 1)], 0)

def primal_part(primal_pack, tile_real, tile_imag):
    stacked = jnp.concatenate([tile_real, tile_imag], 1)
    return jnp.dot(primal_pack, stacked.T, preferred_element_type=jnp.float32)

def adjoint_part(adjoint_pack, tile_real, tile_imag):
    stacked = jnp.concatenate([tile_real, tile_imag], 0)
    return jnp.dot(adjoint_pack, stacked, preferred_element_type=jnp.float32)

def reference(slab_vertices, slab_elements, source_vertices, source_elements, primal_basis, adjoint_basis):
    slab_points = geometry(slab_vertices, slab_elements)
    source_points = geometry(source_vertices, source_elements)
    block_count = SOURCES // SRC_DEV
    source_blocks = source_points.reshape(4, block_count, SRC_DEV).transpose(1, 0, 2)
    basis_blocks = primal_basis.reshape(2 * BASIS, block_count, SRC_DEV).transpose(1, 0, 2)
    adjoint_pack = pack_adjoint(adjoint_basis)

    def advance(running, blocked):
        points, columns = blocked
        tile_real, tile_imag = kernel_tile(slab_points, points)
        running = running + primal_part(pack_primal(columns), tile_real, tile_imag)
        return (running, adjoint_part(adjoint_pack, tile_real, tile_imag))
    summed, adjoint_blocks = lax.scan(advance, jnp.zeros((2 * BASIS, SLAB), jnp.float32), (source_blocks, basis_blocks))
    adjoint_image = adjoint_blocks.transpose(1, 0, 2).reshape(2 * BASIS, SOURCES)
    return (summed, adjoint_image)
```

```python
import math

import jax
import jax.numpy as jnp
from jax import lax
from jax.sharding import PartitionSpec as P

WAVENUMBER = 40.0
SOFTENING = 0.0004
AREA_WEIGHT = 0.05
FOUR_PI = 4.0 * math.pi


def geometry(vertices, elements, anchor):
    local_ids = elements - anchor
    corners = [jnp.take(vertices, local_ids[corner], axis=1) for corner in range(3)]
    centre = (corners[0] + corners[1] + corners[2]) / 3.0
    edge_one = corners[1] - corners[0]
    edge_two = corners[2] - corners[0]
    normal_x = edge_one[1] * edge_two[2] - edge_one[2] * edge_two[1]
    normal_y = edge_one[2] * edge_two[0] - edge_one[0] * edge_two[2]
    normal_z = edge_one[0] * edge_two[1] - edge_one[1] * edge_two[0]
    areas = 0.5 * jnp.sqrt(normal_x * normal_x + normal_y * normal_y + normal_z * normal_z)
    return jnp.concatenate([centre, areas[None, :]], axis=0)


def kernel_tile(targets, sources):
    spread = targets[0][:, None] - sources[0][None, :]
    square_sum = spread * spread
    for axis_id in range(1, 3):
        spread = targets[axis_id][:, None] - sources[axis_id][None, :]
        square_sum = square_sum + spread * spread
    radius = jnp.sqrt(
        square_sum + SOFTENING + AREA_WEIGHT * (targets[3][:, None] + sources[3][None, :])
    )
    weight = targets[3][:, None] * sources[3][None, :] / (FOUR_PI * radius)
    phases = WAVENUMBER * radius
    return (
        (weight * jnp.cos(phases)).astype(jnp.bfloat16),
        (weight * jnp.sin(phases)).astype(jnp.bfloat16),
    )


def pack_primal(columns):
    half_rows = columns.shape[0] // 2
    real_part = columns[:half_rows]
    imag_part = columns[half_rows:]
    return jnp.concatenate(
        [jnp.concatenate([real_part, -imag_part], 1), jnp.concatenate([imag_part, real_part], 1)], 0
    )


def pack_adjoint(row_block):
    half_rows = row_block.shape[0] // 2
    real_part = row_block[:half_rows]
    imag_part = row_block[half_rows:]
    return jnp.concatenate(
        [jnp.concatenate([real_part, imag_part], 1), jnp.concatenate([imag_part, -real_part], 1)], 0
    )


def primal_part(primal_pack, tile_real, tile_imag):
    stacked = jnp.concatenate([tile_real, tile_imag], 1)
    return lax.dot_general(
        primal_pack, stacked, (((1,), (1,)), ((), ())), preferred_element_type=jnp.float32
    )


def adjoint_part(adjoint_pack, tile_real, tile_imag):
    stacked = jnp.concatenate([tile_real, tile_imag], 0)
    return jnp.dot(adjoint_pack, stacked, preferred_element_type=jnp.float32)


def shards(
    slab_vertices, slab_elements, source_vertices, source_elements, primal_basis, adjoint_basis
):
    slab_width = slab_elements.shape[1]
    source_width = source_elements.shape[1]
    wide_at = lax.axis_index("wide")
    flat_at = wide_at * lax.axis_size("long") + lax.axis_index("long")
    slab_points = geometry(slab_vertices, slab_elements, wide_at * (slab_width // 2))
    source_points = geometry(source_vertices, source_elements, flat_at * (source_width // 2))
    gathered_points = lax.all_gather(source_points, "wide", axis=1, tiled=True)
    gathered_basis = lax.all_gather(primal_basis, "wide", axis=1, tiled=True)
    tile_real, tile_imag = kernel_tile(slab_points, gathered_points)
    primal_acc = primal_part(pack_primal(gathered_basis), tile_real, tile_imag)
    adjoint_acc = adjoint_part(pack_adjoint(adjoint_basis), tile_real, tile_imag)
    primal_image = lax.psum_scatter(primal_acc, "long", scatter_dimension=1, tiled=True)
    adjoint_image = lax.psum_scatter(adjoint_acc, "wide", scatter_dimension=1, tiled=True)
    return (primal_image, adjoint_image)


def solution(mesh):
    return jax.shard_map(
        shards,
        mesh=mesh,
        in_specs=(
            P(None, "wide"),
            P(None, "wide"),
            P(None, ("wide", "long")),
            P(None, ("wide", "long")),
            P(None, ("wide", "long")),
            P(None, "wide"),
        ),
        out_specs=(P(None, ("wide", "long")), P(None, ("wide", "long"))),
        check_vma=False,
    )
```
